256 devices in a mesh: segment: 4 (over x), seq: 16 (over z, y_hi), mp: 4 (over y_lo, core).
Axes of the slice: x: 4, y: 4 (y_hi: 2, y_lo: 2; y = y_hi * 2 + y_lo), z: 8, core: 2. Of those that a mesh axis runs over, the one named last changes fastest.
Arguments:
- captions: bfloat16 [16, 128, 4096], P('seq', None, 'segment'), may hold values from -6 to 6
- caption_lengths: int32 [16], replicated, may hold values from 1 to 128, as said below
- image_caption: int32 [16], replicated, may hold values from 0 to 15, each once
- t5_gain: float32 [4096], P('segment'), may hold values from 0.25 to 1.75
- w_key: bfloat16 [4096, 4096], P('segment', 'mp'), may hold values from -0.09375 to 0.09375
- w_value: bfloat16 [4096, 4096], P('segment', 'mp'), may hold values from -0.09375 to 0.09375
- queries: bfloat16 [16, 4096, 4096], P('segment', 'seq', 'mp'), may hold values from -300 to 300
- hidden: bfloat16 [16, 4096, 4096], P('segment', 'seq', 'mp'), may hold values from -1.5 to 1.5
- out_gate: float32 [16, 4096], P('segment', 'mp'), may hold values from 1 to 4
- w_out: bfloat16 [4096, 4096], P('mp', 'seq'), may hold values from -0.09375 to 0.09375
Outputs:
- result_rows: bfloat16 [16, 4096, 4096], P('segment', 'seq', 'mp')
The draws below stay inside these ranges and needn't reach their ends.
Inputs may be any that keep to these rules, and one draw needn't show every extreme that they name: `caption_lengths`: each caption has at least one live token, and some caption fills all 128 slots.
All inputs are finite; a program needn't handle non-finite values.
Results may differ from the reference program's by a relative error of at most 0.03.
Values may be sent and summed in bfloat16 or wider, within the bound.
No kernel may reach another device: no remote copies, remote signals or barrier semaphores. Data moves between devices by JAX's collectives and lax.ppermute only.
A program may use at most 128 MiB of HBM per device.

```python
import jax
import jax.numpy as jnp
from jax import lax

D = 4096
HEADS = 32
HEAD = 128
CAP_LEN = 128
LENGTH = 4096
IMAGES = 16
CAPTIONS = 16
N_MP = 4


def draw_caption_lengths(key, part):
    drawn = jax.random.randint(key, (CAPTIONS,), 1, CAP_LEN + 1)
    longest = jax.random.randint(jax.random.fold_in(key, 7), (), 0, CAPTIONS)
    filled = jnp.where(jnp.arange(CAPTIONS, dtype=jnp.int32) == longest, CAP_LEN, drawn)
    return filled.astype(jnp.int32)


def draw_queries(key, part):
    base = jax.random.normal(key, (IMAGES, LENGTH, D), jnp.float32) * 1.5
    return jnp.clip(base, -300.0, 300.0).astype(jnp.bfloat16)


def steps_of(rng, dims, cuts, low, top_value):
    level = 1.0
    for position, parts in cuts:
        steps = jax.random.uniform(jax.random.fold_in(jax.random.fold_in(rng, 6), position), (parts,), jnp.float32, low / len(cuts), top_value / len(cuts))
        level = level * jnp.repeat(jnp.exp(steps), dims[position] // parts).reshape((-1,) + (1,) * (len(dims) - 1 - position))
    return level


def noise(stream_key, dims, scale, reach, cuts=(), held_as=jnp.bfloat16):
    loudness = steps_of(stream_key, dims, cuts, -0.22, 0.18) if cuts else 1.0
    array = jax.random.normal(stream_key, dims, jnp.float32) * scale * loudness
    return jnp.minimum(jnp.maximum(array, -reach), reach).astype(held_as)


def setup_inputs(seed: int = 0) -> dict:
    seeds = jax.random.split(jax.random.key(seed), 11)
    captions = noise(seeds[0], (CAPTIONS, CAP_LEN, D), 1.0, 6.0, ((0, 16), (2, 4)))
    caption_lengths = draw_caption_lengths(jax.random.fold_in(seeds[10], 71), 0)
    image_caption = jax.random.permutation(seeds[2], IMAGES).astype(jnp.int32)
    t5_gain = jnp.clip(1.0 + 0.15 * jax.random.normal(seeds[3], (D,), jnp.float32), 0.25, 1.75)
    w_key = noise(seeds[4], (D, D), D ** -0.5, 0.09375, ((0, 4), (1, 4)))
    w_value = noise(seeds[5], (D, D), D ** -0.5, 0.09375, ((0, 4), (1, 4)))
    queries = draw_queries(jax.random.fold_in(seeds[10], 71), 0)
    hidden = noise(seeds[7], (IMAGES, LENGTH, D), 0.25, 1.5, ((0, 4), (1, 16), (2, 4)))
    out_gate = jnp.clip(1.0 + 3.0 * jax.random.uniform(seeds[8], (IMAGES, D), jnp.float32) ** steps_of(seeds[8], (IMAGES, D), ((0, 4), (1, 4)), -0.2, 0.2), 1.0, 4.0)
    w_out = noise(seeds[9], (D, D), D ** -0.5, 0.09375, ((0, 4), (1, 16)))
    return {"captions": captions, "caption_lengths": caption_lengths, "image_caption": image_caption, "t5_gain": t5_gain, "w_key": w_key, "w_value": w_value, "queries": queries, "hidden": hidden, "out_gate": out_gate, "w_out": w_out}


def reference(captions, caption_lengths, image_caption, t5_gain, w_key, w_value, queries, hidden, out_gate, w_out):
    caption_values = captions.astype(jnp.float32)
    mean_square = lax.optimization_barrier(jnp.mean(caption_values * caption_values, axis=2, keepdims=True))
    normed = (caption_values * lax.rsqrt(mean_square + 1e-06) * t5_gain).astype(jnp.bfloat16)
    flattened = normed.reshape(CAPTIONS * CAP_LEN, D)
    key_rows = jnp.dot(flattened, w_key, preferred_element_type=jnp.float32).astype(jnp.bfloat16).reshape(CAPTIONS, CAP_LEN, D)
    value_rows = jnp.dot(flattened, w_value, preferred_element_type=jnp.float32).astype(jnp.bfloat16).reshape(CAPTIONS, CAP_LEN, D)
    group_width = D // N_MP

    def per_image(image):
        caption = image_caption[image]
        key_heads = jnp.take(key_rows, caption, axis=0).reshape(CAP_LEN, HEADS, HEAD).astype(jnp.float32)
        value_heads = jnp.take(value_rows, caption, axis=0).reshape(CAP_LEN, HEADS, HEAD).astype(jnp.float32)
        query_heads = jnp.take(queries, image, axis=0).reshape(LENGTH, HEADS, HEAD).astype(jnp.float32)
        scores = jnp.einsum('phd,khd->hpk', query_heads, key_heads) * HEAD ** (-0.5)
        live_mask = jnp.arange(CAP_LEN, dtype=jnp.int32) < jnp.take(caption_lengths, caption)
        scores = jnp.where(live_mask[None, None, :], scores, -1e+30)
        weights = jax.nn.softmax(scores, axis=2).astype(jnp.bfloat16)
        attended = jnp.einsum('hpk,khd->phd', weights.astype(jnp.float32), value_heads)
        attended = attended.astype(jnp.bfloat16).reshape(LENGTH, D)
        projected = jnp.zeros((LENGTH, D), jnp.float32)
        for group in range(N_MP):
            partial_value = jnp.dot(attended[:, group * group_width:(group + 1) * group_width], w_out[group * group_width:(group + 1) * group_width], preferred_element_type=jnp.float32)
            projected = projected + lax.optimization_barrier(partial_value.astype(jnp.bfloat16)).astype(jnp.float32)
        gate_row = jnp.take(out_gate, image, axis=0)
        residual = jnp.take(hidden, image, axis=0).astype(jnp.float32)
        return (residual + gate_row[None, :] * projected).astype(jnp.bfloat16)
    return lax.map(per_image, jnp.arange(IMAGES, dtype=jnp.int32))
```

```python
import functools
import math

import jax
import jax.numpy as jnp
from jax import lax
from jax.experimental import pallas as pl
from jax.experimental.pallas import tpu as pltpu
from jax.sharding import Mesh
from jax.sharding import PartitionSpec as P

HEAD = 128
SEQ = ("z", "yh")
MP = ("yl", "core")
SWAP = [(0, 1), (1, 0)]
VMEM = pl.BlockSpec(memory_space=pltpu.VMEM)
SMEM = pl.BlockSpec(memory_space=pltpu.SMEM)
PARAMS = pltpu.CompilerParams(vmem_limit_bytes=48 * 1024 * 1024)
F32 = jnp.float32
BF16 = jnp.bfloat16


def rotation(count, by):
    return [(k, (k + by) % count) for k in range(count)]


def cost(flops, moved):
    return pl.CostEstimate(flops=flops, bytes_accessed=moved, transcendentals=0)


def project_kernel(nx, owner_ref, pieces_ref, gain_ref, wk_ref, wv_ref, *rest):
    outs, scratch = rest[:nx], rest[nx]
    captions, slots, share = pieces_ref.shape
    cols = wk_ref.shape[1]
    rows = pieces_ref[...].reshape(captions * slots, share).astype(F32)
    squares = jnp.sum(rows * rows, axis=1, keepdims=True)
    high = squares.astype(BF16).astype(F32)
    low = squares - high
    lane = lax.broadcasted_iota(jnp.int32, (captions * slots, HEAD), 1)
    tail = jnp.where(lane == 0, high, jnp.where(lane == 1, low, 0.0))
    scratch[:, 2 * cols :] = tail.astype(BF16)
    scaled = (rows * gain_ref[...]).astype(BF16)
    scratch[:, :cols] = jnp.dot(scaled, wk_ref[...], preferred_element_type=F32).astype(BF16)
    scratch[:, cols : 2 * cols] = jnp.dot(
        scaled, wv_ref[...], preferred_element_type=F32
    ).astype(BF16)
    x = lax.axis_index("x")
    images = outs[0].shape[0]
    for r in range(nx):
        there = lax.rem(x + r, nx)
        for j in range(images):
            caption = owner_ref[there * images + j]
            start = pl.multiple_of(caption * slots, slots)
            outs[r][j] = scratch[pl.ds(start, slots), :]


def add_kernel(width, *refs):
    parts, outs = refs[:-2], refs[-2:]
    images, slots, wide = parts[0].shape
    cols = (wide - HEAD) // 2
    total = parts[0][...].astype(F32)
    for p in parts[1:]:
        total = total + p[...].astype(F32)
    squares = total[:, :, 2 * cols : 2 * cols + 1] + total[:, :, 2 * cols + 1 : 2 * cols + 2]
    scale = lax.rsqrt(squares / width + 1e-06)
    keys = total[:, :, :cols] * (scale * (HEAD**-0.5 * math.log2(math.e)))
    values = total[:, :, cols : 2 * cols] * scale
    half = images // 2
    for s in range(2):
        outs[s][:, :, :cols] = keys[s * half : (s + 1) * half].astype(BF16)
        outs[s][:, :, cols:] = values[s * half : (s + 1) * half].astype(BF16)


def attend_kernel(image, images, nz, owner_ref, length_ref, mine_ref, theirs_ref, *rest):
    pieces, (keep_ref, send_ref) = rest[:nz], rest[nz:]
    core, z = lax.axis_index("core"), lax.axis_index("z")
    rows, cols = mine_ref.shape[1:]
    slots = pieces[0].shape[1]
    live = length_ref[owner_ref[lax.axis_index("x") * images + image]]
    lane = lax.broadcasted_iota(jnp.int32, (2 * rows, HEAD), 1)
    slot = lax.rem(z + nz - lane // slots, nz) * slots + lax.rem(lane, slots)
    dead = slot >= live
    for h in range(cols // HEAD):
        at = slice(h * HEAD, (h + 1) * HEAD)
        there = slice(cols + h * HEAD, cols + (h + 1) * HEAD)
        mine, theirs = mine_ref[0, :, at], theirs_ref[0, :, at]
        q = jnp.concatenate(
            [jnp.where(core == 0, mine, theirs), jnp.where(core == 0, theirs, mine)], axis=0
        )
        keys = jnp.concatenate([p[0, :, at] for p in pieces], axis=0)
        values = jnp.concatenate([p[0, :, there] for p in pieces], axis=0)
        scores = lax.dot_general(q, keys, (((1,), (1,)), ((), ())), preferred_element_type=F32)
        scores = jnp.where(dead, -1e30, scores)
        top = jnp.max(scores, axis=1, keepdims=True)
        raised = jnp.exp2(scores - top)
        weights = (raised / jnp.sum(raised, axis=1, keepdims=True)).astype(BF16)
        out = jnp.dot(weights, values, preferred_element_type=F32).astype(BF16)
        keep_ref[:, at] = out[:rows]
        send_ref[:, at] = out[rows:]


def output_kernel(nx, nz, keep_ref, come_ref, *rest):
    mine, theirs = rest[:nx], rest[nx : 2 * nx]
    send_ref, stay_ref = rest[2 * nx :]
    x, z = lax.axis_index("x"), lax.axis_index("z")
    core, yl = lax.axis_index("core"), lax.axis_index("yl")
    deep, wide = mine[0].shape[1:]
    sent_block = jnp.where(core == 0, 1 - yl, yl)
    slabs = []
    for ref in (keep_ref, come_ref):
        for r in range(nx):
            start = pl.multiple_of(lax.rem(x + nx - r, nx) * deep, deep)
            slabs.append(ref[:, pl.ds(start, deep)])
    left = jnp.concatenate(slabs, axis=1)
    half = nz // 2
    for k in range(nz):
        right = jnp.concatenate([w[k] for w in (*mine, *theirs)], axis=0)
        out = jnp.dot(left, right, preferred_element_type=F32).astype(BF16)
        there = lax.rem(z + nz - k, nz)
        start = pl.multiple_of(lax.rem(there, half) * wide, wide)

        @pl.when(there // half == sent_block)
        def _():
            send_ref[:, pl.ds(start, wide)] = out

        @pl.when(there // half != sent_block)
        def _():
            stay_ref[:, pl.ds(start, wide)] = out


def combine_kernel(stay_ref, come_ref, a_ref, b_ref):
    core = lax.axis_index("core")
    half = a_ref.shape[1]
    for ref, which in ((a_ref, 1 - core), (b_ref, core)):
        at = pl.ds(pl.multiple_of(which * half, half), half)
        ref[...] = (stay_ref[:, at].astype(F32) + come_ref[:, at].astype(F32)).astype(BF16)


def finish_kernel(image, hidden_ref, gate_ref, a_ref, b_ref, *rest):
    out_ref = rest[-1]
    core, yh = lax.axis_index("core"), lax.axis_index("yh")
    second = lax.rem(yh + core, 2)
    wide = a_ref.shape[1] // 2
    for ref, parity in ((a_ref, 1 - second), (b_ref, second)):
        for k in range(2):
            at = pl.ds(pl.multiple_of((2 * k + parity) * wide, wide), wide)
            part = ref[:, k * wide : (k + 1) * wide].astype(F32)
            out = hidden_ref[0, :, at].astype(F32) + gate_ref[image : image + 1, at] * part
            out_ref[0, :, at] = out.astype(BF16)


def shards(
    captions,
    caption_lengths,
    image_caption,
    t5_gain,
    w_key,
    w_value,
    queries,
    hidden,
    out_gate,
    w_out,
):
    nx, nz, nh = lax.axis_size("x"), lax.axis_size("z"), lax.axis_size("yh")
    _, slots, share = captions.shape
    images, rows, cols = queries.shape
    deep, wide = w_out.shape
    slot_share = slots // nz
    caption_count = nz * nh

    cut = captions.reshape(nz, 1, slot_share, share)
    cut = jnp.broadcast_to(cut, (nz, nh, slot_share, share))
    cut = cut.reshape(caption_count, slot_share, share)
    pieces = lax.all_to_all(cut, SEQ, 0, 0, tiled=True)

    theirs = lax.ppermute(queries, "yh", SWAP)

    quarter = deep // nx
    mine = lax.dynamic_slice_in_dim(w_out, lax.axis_index("x") * quarter, quarter, 0)
    over_z = [mine] + [lax.ppermute(mine, "z", rotation(nz, k)) for k in range(1, nz)]
    over_z = jnp.stack(over_z)
    w_mine = [over_z] + [lax.ppermute(over_z, "x", rotation(nx, r)) for r in range(1, nx)]
    w_theirs = [lax.ppermute(w, "core", SWAP) for w in w_mine]

    partial = pl.pallas_call(
        functools.partial(project_kernel, nx),
        name="project",
        out_shape=[jax.ShapeDtypeStruct((images, slot_share, 2 * cols + HEAD), BF16)] * nx,
        in_specs=[SMEM, VMEM, VMEM, VMEM, VMEM],
        out_specs=[VMEM] * nx,
        scratch_shapes=[pltpu.VMEM((caption_count * slot_share, 2 * cols + HEAD), BF16)],
        compiler_params=PARAMS,
        cost_estimate=cost(4 * caption_count * slot_share * share * cols, 6 << 20),
    )(image_caption, pieces, t5_gain.reshape(1, share), w_key, w_value)
    arrived = [partial[0]] + [
        lax.ppermute(partial[r], "x", rotation(nx, r)) for r in range(1, nx)
    ]
    streams = pl.pallas_call(
        functools.partial(add_kernel, float(share * nx)),
        name="add",
        out_shape=[jax.ShapeDtypeStruct((images // 2, slot_share, 2 * cols), BF16)] * 2,
        in_specs=[VMEM] * nx,
        out_specs=[VMEM] * 2,
        compiler_params=PARAMS,
        cost_estimate=cost(1 << 20, 2 << 20),
    )(*arrived)
    rings = []
    for stream in streams:
        ring = [stream] + [None] * (nz - 1)
        for k in range(1, nz // 2 + 1):
            ring[k] = lax.ppermute(ring[k - 1], "z", rotation(nz, 1))
            if k < nz - k:
                ring[nz - k] = lax.ppermute(ring[(nz - k + 1) % nz], "z", rotation(nz, -1))
        rings.append(ring)

    across = [(h * 4 + l * 2, h * 4 + l * 2 + 1) for h in range(2) for l in range(2)]
    across += [(h * 4 + l * 2 + 1, (1 - h) * 4 + (1 - l) * 2) for h in range(2) for l in range(2)]
    beside = [(h * 4 + l * 2, h * 4 + l * 2) for h in range(2) for l in range(2)]
    beside += [
        (h * 4 + l * 2 + 1, (1 - h) * 4 + (1 - l) * 2 + 1) for h in range(2) for l in range(2)
    ]

    result = None
    for j in range(images):
        in_stream = j % (images // 2)
        block = pl.BlockSpec((1, rows, cols), lambda i, j=j: (j, 0, 0))
        piece = pl.BlockSpec((1, slot_share, 2 * cols), lambda i, j=in_stream: (j, 0, 0))
        flat = pl.BlockSpec((rows, cols), lambda i: (0, 0))
        keep, send = pl.pallas_call(
            functools.partial(attend_kernel, j, images, nz),
            name="attend",
            grid=(1,),
            out_shape=[jax.ShapeDtypeStruct((rows, cols), BF16)] * 2,
            in_specs=[SMEM, SMEM, block, block] + [piece] * nz,
            out_specs=[flat, flat],
            compiler_params=PARAMS,
            cost_estimate=cost(16 * rows * slots * cols, 3 << 20),
        )(image_caption, caption_lengths, queries, theirs, *rings[j // (images // 2)])
        come = lax.ppermute(send, "core", SWAP)
        out_send, out_stay = pl.pallas_call(
            functools.partial(output_kernel, nx, nz),
            name="output",
            out_shape=[jax.ShapeDtypeStruct((rows, nz // 2 * wide), BF16)] * 2,
            in_specs=[VMEM] * (2 + 2 * nx),
            out_specs=[VMEM] * 2,
            compiler_params=PARAMS,
            cost_estimate=cost(4 * rows * deep * nz * wide, 10 << 20),
        )(keep, come, *w_mine, *w_theirs)
        out_come = lax.ppermute(out_send, "yl", SWAP)
        a, b = pl.pallas_call(
            combine_kernel,
            name="combine",
            out_shape=[jax.ShapeDtypeStruct((rows, cols // 2), BF16)] * 2,
            in_specs=[VMEM] * 2,
            out_specs=[VMEM] * 2,
            compiler_params=PARAMS,
            cost_estimate=cost(1 << 18, 2 << 20),
        )(out_stay, out_come)
        a = lax.ppermute(a, ("yh", "yl", "core"), across)
        b = lax.ppermute(b, ("yh", "yl", "core"), beside)
        before = [] if result is None else [result]
        part = pl.BlockSpec((rows, cols // 2), lambda i: (0, 0))
        result = pl.pallas_call(
            functools.partial(finish_kernel, j),
            name="finish",
            grid=(1,),
            out_shape=jax.ShapeDtypeStruct(hidden.shape, BF16),
            in_specs=[block, pl.BlockSpec(out_gate.shape, lambda i: (0, 0)), part, part]
            + [pl.BlockSpec(memory_space=pl.ANY)] * len(before),
            out_specs=block,
            input_output_aliases={4: 0} if before else {},
            compiler_params=PARAMS,
            cost_estimate=cost(1 << 18, 2 << 20),
        )(hidden, out_gate, a, b, *before)
    return result


def solution(mesh):
    split = Mesh(
        mesh.devices.reshape(mesh.shape["segment"], 8, 2, 2, 2), ("x", "z", "yh", "yl", "core")
    )
    return jax.shard_map(
        shards,
        mesh=split,
        in_specs=(
            P(SEQ, None, "x"),
            P(),
            P(),
            P("x"),
            P("x", MP),
            P("x", MP),
            P("x", SEQ, MP),
            P("x", SEQ, MP),
            P("x", MP),
            P(MP, SEQ),
        ),
        out_specs=P("x", SEQ, MP),
        check_vma=False,
    )
```

```python
import functools
import math

import jax
import jax.numpy as jnp
from jax import lax
from jax.experimental import pallas as pl
from jax.experimental.pallas import tpu as pltpu
from jax.sharding import Mesh
from jax.sharding import PartitionSpec as P

HEAD = 128
SEQ = ("z", "yh")
MP = ("yl", "core")
SWAP = [(0, 1), (1, 0)]
VMEM = pl.BlockSpec(memory_space=pltpu.VMEM)
SMEM = pl.BlockSpec(memory_space=pltpu.SMEM)
PARAMS = pltpu.CompilerParams(vmem_limit_bytes=26 * 1024 * 1024)
F32 = jnp.float32
BF16 = jnp.bfloat16


def rotation(count, by):
    return [(k, (k + by) % count) for k in range(count)]


def after(value, *tokens):
    return lax.optimization_barrier((value, *tokens))[0]


def cost(flops, moved):
    return pl.CostEstimate(flops=flops, bytes_accessed=moved, transcendentals=0)


def ring_of(value, count, *beside):
    half = count // 2
    ring = [value] + [None] * (count - 1)
    for k in range(1, half + 1):
        if k == half:
            ring[k - 1] = after(ring[k - 1], *beside)
        ring[k] = lax.ppermute(ring[k - 1], "z", rotation(count, 1))
        if k < half:
            ring[count - k] = lax.ppermute(ring[(count - k + 1) % count], "z", rotation(count, -1))
    return ring


def project_kernel(nx, owner_ref, pieces_ref, gain_ref, wk_ref, wv_ref, *rest):
    outs, (scaled, scratch) = rest[:nx], rest[nx:]
    captions, slots, share = pieces_ref.shape
    step, steps = pl.program_id(0), pl.num_programs(0)
    block = wk_ref.shape[1]
    cols = (scratch.shape[1] - HEAD) // 2

    @pl.when(step == 0)
    def _():
        rows = pieces_ref[...].reshape(captions * slots, share).astype(F32)
        squares = jnp.sum(rows * rows, axis=1, keepdims=True)
        high = squares.astype(BF16).astype(F32)
        low = squares - high
        lane = lax.broadcasted_iota(jnp.int32, (captions * slots, HEAD), 1)
        tail = jnp.where(lane == 0, high, jnp.where(lane == 1, low, 0.0))
        scratch[:, 2 * cols :] = tail.astype(BF16)
        scaled[...] = (rows * gain_ref[...]).astype(BF16)

    for ref, offset in ((wk_ref, 0), (wv_ref, cols)):
        at = pl.ds(pl.multiple_of(offset + step * block, block), block)
        scratch[:, at] = jnp.dot(scaled[...], ref[...], preferred_element_type=F32).astype(BF16)

    @pl.when(step == steps - 1)
    def _():
        x = lax.axis_index("x")
        images = outs[0].shape[0]
        for r in range(nx):
            there = lax.rem(x + r, nx)
            for j in range(images):
                caption = owner_ref[there * images + j]
                start = pl.multiple_of(caption * slots, slots)
                outs[r][j] = scratch[pl.ds(start, slots), :]


def add_kernel(width, *refs):
    parts, out_ref = refs[:-1], refs[-1]
    wide = parts[0].shape[2]
    cols = (wide - HEAD) // 2
    total = parts[0][...].astype(F32)
    for p in parts[1:]:
        total = total + p[...].astype(F32)
    squares = total[:, :, 2 * cols : 2 * cols + 1] + total[:, :, 2 * cols + 1 : 2 * cols + 2]
    scale = lax.rsqrt(squares / width + 1e-06)
    keys = total[:, :, :cols] * (scale * (HEAD**-0.5 * math.log2(math.e)))
    out_ref[:, :, :cols] = keys.astype(BF16)
    out_ref[:, :, cols:] = (total[:, :, cols : 2 * cols] * scale).astype(BF16)


def attend_kernel(first, total, nz, owner_ref, length_ref, mine_ref, theirs_ref, *rest):
    pieces, (keep_ref, send_ref) = rest[:nz], rest[nz:]
    core, z = lax.axis_index("core"), lax.axis_index("z")
    rows, cols = mine_ref.shape[1:]
    slots = pieces[0].shape[1]
    image = lax.axis_index("x") * total + first + pl.program_id(0)
    live = length_ref[owner_ref[image]]
    lane = lax.broadcasted_iota(jnp.int32, (2 * rows, HEAD), 1)
    slot = lax.rem(z + nz - lane // slots, nz) * slots + lax.rem(lane, slots)
    dead = slot >= live

    for h in range(cols // HEAD):
        at = slice(h * HEAD, (h + 1) * HEAD)
        there = slice(cols + h * HEAD, cols + (h + 1) * HEAD)
        mine, theirs = mine_ref[0, :, at], theirs_ref[0, :, at]
        q = jnp.concatenate(
            [jnp.where(core == 0, mine, theirs), jnp.where(core == 0, theirs, mine)], axis=0
        )
        keys = jnp.concatenate([p[0, :, at] for p in pieces], axis=0)
        values = jnp.concatenate([p[0, :, there] for p in pieces], axis=0)
        scores = lax.dot_general(q, keys, (((1,), (1,)), ((), ())), preferred_element_type=F32)
        scores = jnp.where(dead, -1e30, scores)
        top = jnp.max(scores, axis=1, keepdims=True)
        raised = jnp.exp2(scores - top)
        weights = (raised / jnp.sum(raised, axis=1, keepdims=True)).astype(BF16)
        out = jnp.dot(weights, values, preferred_element_type=F32).astype(BF16)
        keep_ref[:, at] = out[:rows]
        send_ref[:, at] = out[rows:]


def output_kernel(nx, nz, order_ref, keep_ref, come_ref, *rest):
    sides, outs, (held, sems) = (rest[:5], rest[5:10]), rest[10:-2], rest[-2:]
    sends, stays = outs[: len(outs) // 2], outs[len(outs) // 2 :]
    x = lax.axis_index("x")
    core, yl = lax.axis_index("core"), lax.axis_index("yl")
    deep, wide = rest[0].shape[1:]
    sent_block = jnp.where(core == 0, 1 - yl, yl)
    half = nz // 2

    copies = []
    for first in range(2):
        span = pl.ds(first * half, half)
        group = []
        for side in range(2):
            for part in range(nx):
                ref = sides[side][part].at[span] if part < nx - 1 else sides[side][part + first]
                row = pl.ds((side * nx + part) * deep, deep)
                group.append(
                    pltpu.make_async_copy(ref, held.at[span, row], sems.at[first, side, part])
                )
        copies.append(group)
    for group in copies:
        for copy in group:
            copy.start()

    slabs = []
    for ref in (keep_ref, come_ref):
        for r in (0, 1, nx - 1, 2):
            start = pl.multiple_of(lax.rem(x + nx - r, nx) * deep, deep)
            slabs.append(ref[:, pl.ds(start, deep)])
    left = jnp.concatenate(slabs, axis=1)

    def column(k):
        out = jnp.dot(left, held[k], preferred_element_type=F32).astype(BF16)
        there = k
        start = pl.multiple_of(lax.rem(there, half) * wide, wide)

        rows = sends[0].shape[0]

        @pl.when(there // half == sent_block)
        def _():
            for i, ref in enumerate(sends):
                ref[:, pl.ds(start, wide)] = out[i * rows : (i + 1) * rows]

        @pl.when(there // half != sent_block)
        def _():
            for i, ref in enumerate(stays):
                ref[:, pl.ds(start, wide)] = out[i * rows : (i + 1) * rows]

    for first in range(2):
        for copy in copies[first]:
            copy.wait()

        @pl.loop(0, half)
        def _(k):
            column(first * half + k)


def combine_kernel(stay_ref, come_ref, a_ref, b_ref):
    core = lax.axis_index("core")
    half = a_ref.shape[1]
    for ref, which in ((a_ref, 1 - core), (b_ref, core)):
        at = pl.ds(pl.multiple_of(which * half, half), half)
        ref[...] = (stay_ref[:, at].astype(F32) + come_ref[:, at].astype(F32)).astype(BF16)


def finish_kernel(image, hidden_ref, gate_ref, a_ref, b_ref, *rest):
    out_ref = rest[-1]
    core, yh = lax.axis_index("core"), lax.axis_index("yh")
    second = lax.rem(yh + core, 2)
    wide = a_ref.shape[1] // 2
    for ref, parity in ((a_ref, 1 - second), (b_ref, second)):
        for k in range(2):
            at = pl.ds(pl.multiple_of((2 * k + parity) * wide, wide), wide)
            part = ref[:, k * wide : (k + 1) * wide].astype(F32)
            out = hidden_ref[0, :, at].astype(F32) + gate_ref[image : image + 1, at] * part
            out_ref[0, :, at] = out.astype(BF16)


def shards(
    captions,
    caption_lengths,
    image_caption,
    t5_gain,
    w_key,
    w_value,
    queries,
    hidden,
    out_gate,
    w_out,
):
    nx, nz, nh = lax.axis_size("x"), lax.axis_size("z"), lax.axis_size("yh")
    _, slots, share = captions.shape
    images, rows, cols = queries.shape
    deep, wide = w_out.shape
    slot_share = slots // nz
    caption_count = nz * nh

    cut = captions.reshape(nz, 1, slot_share, share)
    cut = jnp.broadcast_to(cut, (nz, nh, slot_share, share))
    cut = cut.reshape(caption_count, slot_share, share)
    pieces = lax.all_to_all(cut, SEQ, 0, 0, tiled=True)

    theirs = lax.ppermute(after(queries, cut), "yh", SWAP)
    quarter = deep // nx
    mine = lax.dynamic_slice_in_dim(
        after(w_out, cut), lax.axis_index("x") * quarter, quarter, 0
    )
    w_z = lax.all_to_all(
        jnp.broadcast_to(mine[None], (nz, *mine.shape)), "z", 0, 0, tiled=True
    )

    partial = pl.pallas_call(
        functools.partial(project_kernel, nx),
        name="project",
        grid=(4,),
        out_shape=[jax.ShapeDtypeStruct((images, slot_share, 2 * cols + HEAD), BF16)] * nx,
        in_specs=[
            SMEM,
            pl.BlockSpec(pieces.shape, lambda i: (0, 0, 0)),
            pl.BlockSpec((1, share), lambda i: (0, 0)),
            pl.BlockSpec((share, cols // 4), lambda i: (0, i)),
            pl.BlockSpec((share, cols // 4), lambda i: (0, i)),
        ],
        out_specs=[
            pl.BlockSpec((images, slot_share, 2 * cols + HEAD), lambda i: (0, 0, 0))
        ]
        * nx,
        scratch_shapes=[
            pltpu.VMEM((caption_count * slot_share, share), BF16),
            pltpu.VMEM((caption_count * slot_share, 2 * cols + HEAD), BF16),
        ],
        compiler_params=pltpu.CompilerParams(vmem_limit_bytes=58 * 1024 * 1024),
        cost_estimate=cost(4 * caption_count * slot_share * share * cols, 6 << 20),
    )(image_caption, pieces, t5_gain.reshape(1, share), w_key, w_value)
    arrived = [partial[0]] + [
        lax.ppermute(partial[r], "x", rotation(nx, r)) for r in range(1, nx)
    ]
    stream = pl.pallas_call(
        functools.partial(add_kernel, float(share * nx)),
        name="add",
        out_shape=jax.ShapeDtypeStruct((images, slot_share, 2 * cols), BF16),
        in_specs=[VMEM] * nx,
        out_specs=VMEM,
        compiler_params=PARAMS,
        cost_estimate=cost(1 << 16, 1 << 16),
    )(*arrived)
    w_x = after(w_z, stream)
    ahead = lax.ppermute(w_x, "x", rotation(nx, 1))
    back = lax.ppermute(w_x, "x", rotation(nx, -1))
    ring = ring_of(stream, nz, ahead, back)
    far = [
        lax.ppermute(ahead[: nz // 2], "x", rotation(nx, 1)),
        lax.ppermute(back[nz // 2 :], "x", rotation(nx, -1)),
    ]
    w_mine = [w_x, ahead, back, *far]
    w_theirs = [lax.ppermute(w, "core", SWAP) for w in w_mine]

    across = [(h * 4 + l * 2, h * 4 + l * 2 + 1) for h in range(2) for l in range(2)]
    across += [(h * 4 + l * 2 + 1, (1 - h) * 4 + (1 - l) * 2) for h in range(2) for l in range(2)]
    beside = [(h * 4 + l * 2, h * 4 + l * 2) for h in range(2) for l in range(2)]
    beside += [
        (h * 4 + l * 2 + 1, (1 - h) * 4 + (1 - l) * 2 + 1) for h in range(2) for l in range(2)
    ]

    result = None
    batch = images // 2
    for s in range(2):
        block = pl.BlockSpec((1, rows, cols), lambda i, s=s: (s * batch + i, 0, 0))
        piece = pl.BlockSpec((1, slot_share, 2 * cols), lambda i, s=s: (s * batch + i, 0, 0))
        flat = pl.BlockSpec((rows, cols), lambda i: (i, 0))
        keep, send = pl.pallas_call(
            functools.partial(attend_kernel, s * batch, images, nz),
            name="attend",
            grid=(batch,),
            out_shape=[jax.ShapeDtypeStruct((batch * rows, cols), BF16)] * 2,
            in_specs=[SMEM, SMEM, block, block] + [piece] * nz,
            out_specs=[flat, flat],
            compiler_params=PARAMS,
            cost_estimate=cost(1 << 16, 1 << 16),
        )(
            after(image_caption, *far) if s else image_caption,
            caption_lengths,
            queries,
            theirs,
            *ring,
        )
        come = lax.ppermute(send, "core", SWAP)
        outs = pl.pallas_call(
            functools.partial(output_kernel, nx, nz),
            name="output",
            out_shape=[jax.ShapeDtypeStruct((rows, nz // 2 * wide), BF16)] * (2 * batch),
            in_specs=[SMEM, VMEM, VMEM] + [pl.BlockSpec(memory_space=pl.ANY)] * 10,
            out_specs=[VMEM] * (2 * batch),
            scratch_shapes=[
                pltpu.VMEM((nz, 2 * deep, wide), BF16),
                pltpu.SemaphoreType.DMA((2, 2, nx)),
            ],
            compiler_params=PARAMS,
            cost_estimate=cost(1 << 16, 1 << 16),
        )(image_caption, keep, come, *w_mine, *w_theirs)
        for i in range(batch):
            j = s * batch + i
            out_come = lax.ppermute(outs[i], "yl", SWAP)
            a, b = pl.pallas_call(
                combine_kernel,
                name="combine",
                out_shape=[jax.ShapeDtypeStruct((rows, cols // 2), BF16)] * 2,
                in_specs=[VMEM] * 2,
                out_specs=[VMEM] * 2,
                compiler_params=PARAMS,
                cost_estimate=cost(1 << 16, 1 << 16),
            )(outs[batch + i], out_come)
            a = lax.ppermute(a, ("yh", "yl", "core"), across)
            b = lax.ppermute(b, ("yh", "yl", "core"), beside)
            before = [] if result is None else [result]
            part = pl.BlockSpec((rows, cols // 2), lambda i: (0, 0))
            block = pl.BlockSpec((1, rows, cols), lambda i, j=j: (j, 0, 0))
            result = pl.pallas_call(
                functools.partial(finish_kernel, j),
                name="finish",
                grid=(1,),
                out_shape=jax.ShapeDtypeStruct(hidden.shape, BF16),
                in_specs=[block, pl.BlockSpec(out_gate.shape, lambda i: (0, 0)), part, part]
                + [pl.BlockSpec(memory_space=pl.ANY)] * len(before),
                out_specs=block,
                input_output_aliases={4: 0} if before else {},
                compiler_params=PARAMS,
                cost_estimate=cost(1 << 16, 1 << 16),
            )(hidden, out_gate, a, b, *before)
    return result


def solution(mesh):
    split = Mesh(
        mesh.devices.reshape(mesh.shape["segment"], 8, 2, 2, 2), ("x", "z", "yh", "yl", "core")
    )
    return jax.shard_map(
        shards,
        mesh=split,
        in_specs=(
            P(SEQ, None, "x"),
            P(),
            P(),
            P("x"),
            P("x", MP),
            P("x", MP),
            P("x", SEQ, MP),
            P("x", SEQ, MP),
            P("x", MP),
            P(MP, SEQ),
        ),
        out_specs=P("x", SEQ, MP),
        check_vma=False,
    )
```

```python
import functools
import math

import jax
import jax.numpy as jnp
from jax import lax
from jax.experimental import pallas as pl
from jax.experimental.pallas import tpu as pltpu
from jax.sharding import Mesh
from jax.sharding import PartitionSpec as P

HEAD = 128
SEQ = ("z", "yh")
MP = ("yl", "core")
SWAP = [(0, 1), (1, 0)]
VMEM = pl.BlockSpec(memory_space=pltpu.VMEM)
SMEM = pl.BlockSpec(memory_space=pltpu.SMEM)
PARAMS = pltpu.CompilerParams(vmem_limit_bytes=26 * 1024 * 1024)
F32 = jnp.float32
BF16 = jnp.bfloat16


def rotation(count, by):
    return [(k, (k + by) % count) for k in range(count)]


def after(value, *tokens):
    return lax.optimization_barrier((value, *tokens))[0]


def cost(flops, moved):
    return pl.CostEstimate(flops=flops, bytes_accessed=moved, transcendentals=0)


def ring_of(value, count, *beside):
    half = count // 2
    ring = [value] + [None] * (count - 1)
    for k in range(1, half + 1):
        if k == half:
            ring[k - 1] = after(ring[k - 1], *beside)
        ring[k] = lax.ppermute(ring[k - 1], "z", rotation(count, 1))
        if k < half:
            ring[count - k] = lax.ppermute(ring[(count - k + 1) % count], "z", rotation(count, -1))
    return ring


def project_kernel(nx, owner_ref, pieces_ref, gain_ref, wk_ref, wv_ref, *rest):
    outs, (scaled, scratch) = rest[:nx], rest[nx:]
    captions, slots, share = pieces_ref.shape
    step, steps = pl.program_id(0), pl.num_programs(0)
    block = wk_ref.shape[1]
    cols = (scratch.shape[1] - HEAD) // 2

    @pl.when(step == 0)
    def _():
        rows = pieces_ref[...].reshape(captions * slots, share).astype(F32)
        squares = jnp.sum(rows * rows, axis=1, keepdims=True)
        high = squares.astype(BF16).astype(F32)
        low = squares - high
        lane = lax.broadcasted_iota(jnp.int32, (captions * slots, HEAD), 1)
        tail = jnp.where(lane == 0, high, jnp.where(lane == 1, low, 0.0))
        scratch[:, 2 * cols :] = tail.astype(BF16)
        scaled[...] = (rows * gain_ref[...]).astype(BF16)

    for ref, offset in ((wk_ref, 0), (wv_ref, cols)):
        at = pl.ds(pl.multiple_of(offset + step * block, block), block)
        scratch[:, at] = jnp.dot(scaled[...], ref[...], preferred_element_type=F32).astype(BF16)

    @pl.when(step == steps - 1)
    def _():
        x = lax.axis_index("x")
        images = outs[0].shape[0]
        for r in range(nx):
            there = lax.rem(x + r, nx)
            for j in range(images):
                caption = owner_ref[there * images + j]
                start = pl.multiple_of(caption * slots, slots)
                outs[r][j] = scratch[pl.ds(start, slots), :]


def add_kernel(width, *refs):
    parts, out_ref = refs[:-1], refs[-1]
    wide = parts[0].shape[2]
    cols = (wide - HEAD) // 2
    total = parts[0][...].astype(F32)
    for p in parts[1:]:
        total = total + p[...].astype(F32)
    squares = total[:, :, 2 * cols : 2 * cols + 1] + total[:, :, 2 * cols + 1 : 2 * cols + 2]
    scale = lax.rsqrt(squares / width + 1e-06)
    keys = total[:, :, :cols] * (scale * (HEAD**-0.5 * math.log2(math.e)))
    out_ref[:, :, :cols] = keys.astype(BF16)
    out_ref[:, :, cols:] = (total[:, :, cols : 2 * cols] * scale).astype(BF16)


def attend_kernel(first, total, nz, owner_ref, length_ref, mine_ref, theirs_ref, *rest):
    pieces, (keep_ref, send_ref) = rest[:nz], rest[nz:]
    core, z = lax.axis_index("core"), lax.axis_index("z")
    rows, cols = mine_ref.shape[1:]
    slots = pieces[0].shape[1]
    image = lax.axis_index("x") * total + first + pl.program_id(0)
    live = length_ref[owner_ref[image]]
    lane = lax.broadcasted_iota(jnp.int32, (2 * rows, HEAD), 1)
    slot = lax.rem(z + nz - lane // slots, nz) * slots + lax.rem(lane, slots)
    dead = slot >= live

    for h in range(cols // HEAD):
        at = slice(h * HEAD, (h + 1) * HEAD)
        there = slice(cols + h * HEAD, cols + (h + 1) * HEAD)
        mine, theirs = mine_ref[0, :, at], theirs_ref[0, :, at]
        q = jnp.concatenate(
            [jnp.where(core == 0, mine, theirs), jnp.where(core == 0, theirs, mine)], axis=0
        )
        keys = jnp.concatenate([p[0, :, at] for p in pieces], axis=0)
        values = jnp.concatenate([p[0, :, there] for p in pieces], axis=0)
        scores = lax.dot_general(q, keys, (((1,), (1,)), ((), ())), preferred_element_type=F32)
        scores = jnp.where(dead, -1e30, scores)
        top = jnp.max(scores, axis=1, keepdims=True)
        raised = jnp.exp2(scores - top)
        weights = (raised / jnp.sum(raised, axis=1, keepdims=True)).astype(BF16)
        out = jnp.dot(weights, values, preferred_element_type=F32).astype(BF16)
        keep_ref[:, at] = out[:rows]
        send_ref[:, at] = out[rows:]


def output_kernel(nx, nz, order_ref, keep_ref, come_ref, *rest):
    sides, outs, (held, sems) = (rest[:5], rest[5:10]), rest[10:-2], rest[-2:]
    sends, stays = outs[: len(outs) // 2], outs[len(outs) // 2 :]
    x = lax.axis_index("x")
    core, yl = lax.axis_index("core"), lax.axis_index("yl")
    deep, wide = rest[0].shape[1:]
    sent_block = jnp.where(core == 0, 1 - yl, yl)
    half = nz // 2

    copies = []
    for first in range(2):
        span = pl.ds(first * half, half)
        group = []
        for side in range(2):
            for part in range(nx):
                ref = sides[side][part].at[span] if part < nx - 1 else sides[side][part + first]
                row = pl.ds((side * nx + part) * deep, deep)
                group.append(
                    pltpu.make_async_copy(ref, held.at[span, row], sems.at[first, side, part])
                )
        copies.append(group)
    for group in copies:
        for copy in group:
            copy.start()

    slabs = []
    for ref in (keep_ref, come_ref):
        for r in (0, 1, nx - 1, 2):
            start = pl.multiple_of(lax.rem(x + nx - r, nx) * deep, deep)
            slabs.append(ref[:, pl.ds(start, deep)])
    left = jnp.concatenate(slabs, axis=1)

    def column(k):
        out = jnp.dot(left, held[k], preferred_element_type=F32).astype(BF16)
        there = k
        start = pl.multiple_of(lax.rem(there, half) * wide, wide)

        rows = sends[0].shape[0]

        @pl.when(there // half == sent_block)
        def _():
            for i, ref in enumerate(sends):
                ref[:, pl.ds(start, wide)] = out[i * rows : (i + 1) * rows]

        @pl.when(there // half != sent_block)
        def _():
            for i, ref in enumerate(stays):
                ref[:, pl.ds(start, wide)] = out[i * rows : (i + 1) * rows]

    for first in range(2):
        for copy in copies[first]:
            copy.wait()

        @pl.loop(0, half)
        def _(k):
            column(first * half + k)


def combine_kernel(stay_ref, come_ref, a_ref, b_ref):
    core = lax.axis_index("core")
    half = a_ref.shape[1]
    for ref, which in ((a_ref, 1 - core), (b_ref, core)):
        at = pl.ds(pl.multiple_of(which * half, half), half)
        ref[...] = (stay_ref[:, at].astype(F32) + come_ref[:, at].astype(F32)).astype(BF16)


def finish_kernel(image, hidden_ref, gate_ref, a_ref, b_ref, *rest):
    out_ref = rest[-1]
    core, yh = lax.axis_index("core"), lax.axis_index("yh")
    second = lax.rem(yh + core, 2)
    wide = a_ref.shape[1] // 2
    for ref, parity in ((a_ref, 1 - second), (b_ref, second)):
        for k in range(2):
            at = pl.ds(pl.multiple_of((2 * k + parity) * wide, wide), wide)
            part = ref[:, k * wide : (k + 1) * wide].astype(F32)
            out = hidden_ref[0, :, at].astype(F32) + gate_ref[image : image + 1, at] * part
            out_ref[0, :, at] = out.astype(BF16)


def shards(
    captions,
    caption_lengths,
    image_caption,
    t5_gain,
    w_key,
    w_value,
    queries,
    hidden,
    out_gate,
    w_out,
):
    nx, nz, nh = lax.axis_size("x"), lax.axis_size("z"), lax.axis_size("yh")
    _, slots, share = captions.shape
    images, rows, cols = queries.shape
    deep, wide = w_out.shape
    slot_share = slots // nz
    caption_count = nz * nh

    cut = captions.reshape(nz, 1, slot_share, share)
    cut = jnp.broadcast_to(cut, (nz, nh, slot_share, share))
    cut = cut.reshape(caption_count, slot_share, share)
    pieces = lax.all_to_all(cut, SEQ, 0, 0, tiled=True)

    theirs = lax.ppermute(after(queries, cut), "yh", SWAP)
    quarter = deep // nx
    mine = lax.dynamic_slice_in_dim(
        after(w_out, cut), lax.axis_index("x") * quarter, quarter, 0
    )
    w_z = lax.all_to_all(
        jnp.broadcast_to(mine[None], (nz, *mine.shape)), "z", 0, 0, tiled=True
    )

    partial = pl.pallas_call(
        functools.partial(project_kernel, nx),
        name="project",
        grid=(4,),
        out_shape=[jax.ShapeDtypeStruct((images, slot_share, 2 * cols + HEAD), BF16)] * nx,
        in_specs=[
            SMEM,
            pl.BlockSpec(pieces.shape, lambda i: (0, 0, 0)),
            pl.BlockSpec((1, share), lambda i: (0, 0)),
            pl.BlockSpec((share, cols // 4), lambda i: (0, i)),
            pl.BlockSpec((share, cols // 4), lambda i: (0, i)),
        ],
        out_specs=[
            pl.BlockSpec((images, slot_share, 2 * cols + HEAD), lambda i: (0, 0, 0))
        ]
        * nx,
        scratch_shapes=[
            pltpu.VMEM((caption_count * slot_share, share), BF16),
            pltpu.VMEM((caption_count * slot_share, 2 * cols + HEAD), BF16),
        ],
        compiler_params=pltpu.CompilerParams(vmem_limit_bytes=58 * 1024 * 1024),
        cost_estimate=cost(4 * caption_count * slot_share * share * cols, 6 << 20),
    )(image_caption, pieces, t5_gain.reshape(1, share), w_key, w_value)
    arrived = [partial[0]] + [
        lax.ppermute(partial[r], "x", rotation(nx, r)) for r in range(1, nx)
    ]
    stream = pl.pallas_call(
        functools.partial(add_kernel, float(share * nx)),
        name="add",
        out_shape=jax.ShapeDtypeStruct((images, slot_share, 2 * cols), BF16),
        in_specs=[VMEM] * nx,
        out_specs=VMEM,
        compiler_params=PARAMS,
        cost_estimate=cost(1 << 16, 1 << 16),
    )(*arrived)
    w_x = after(w_z, stream)
    ahead = lax.ppermute(w_x, "x", rotation(nx, 1))
    back = lax.ppermute(w_x, "x", rotation(nx, -1))
    ring = ring_of(stream, nz, ahead, back)
    far = [
        lax.ppermute(ahead[: nz // 2], "x", rotation(nx, 1)),
        lax.ppermute(back[nz // 2 :], "x", rotation(nx, -1)),
    ]
    w_mine = [w_x, ahead, back, *far]
    w_theirs = [lax.ppermute(w, "core", SWAP) for w in w_mine]

    across = [(h * 4 + l * 2, h * 4 + l * 2 + 1) for h in range(2) for l in range(2)]
    across += [(h * 4 + l * 2 + 1, (1 - h) * 4 + (1 - l) * 2) for h in range(2) for l in range(2)]
    beside = [(h * 4 + l * 2, h * 4 + l * 2) for h in range(2) for l in range(2)]
    beside += [
        (h * 4 + l * 2 + 1, (1 - h) * 4 + (1 - l) * 2 + 1) for h in range(2) for l in range(2)
    ]

    result, projected = None, []
    batch = images // 2
    for s in range(2):
        block = pl.BlockSpec((1, rows, cols), lambda i, s=s: (s * batch + i, 0, 0))
        piece = pl.BlockSpec((1, slot_share, 2 * cols), lambda i, s=s: (s * batch + i, 0, 0))
        flat = pl.BlockSpec((rows, cols), lambda i: (i, 0))
        keep, send = pl.pallas_call(
            functools.partial(attend_kernel, s * batch, images, nz),
            name="attend",
            grid=(batch,),
            out_shape=[jax.ShapeDtypeStruct((batch * rows, cols), BF16)] * 2,
            in_specs=[SMEM, SMEM, block, block] + [piece] * nz,
            out_specs=[flat, flat],
            compiler_params=PARAMS,
            cost_estimate=cost(1 << 16, 1 << 16),
        )(
            after(image_caption, *far) if s else image_caption,
            caption_lengths,
            queries,
            theirs,
            *ring,
        )
        come = lax.ppermute(send, "core", SWAP)
        outs = pl.pallas_call(
            functools.partial(output_kernel, nx, nz),
            name="output",
            out_shape=[jax.ShapeDtypeStruct((rows, nz // 2 * wide), BF16)] * (2 * batch),
            in_specs=[SMEM, VMEM, VMEM] + [pl.BlockSpec(memory_space=pl.ANY)] * 10,
            out_specs=[VMEM] * (2 * batch),
            scratch_shapes=[
                pltpu.VMEM((nz, 2 * deep, wide), BF16),
                pltpu.SemaphoreType.DMA((2, 2, nx)),
            ],
            compiler_params=PARAMS,
            cost_estimate=cost(1 << 16, 1 << 16),
        )(image_caption, keep, come, *w_mine, *w_theirs)
        projected.append(outs)
    for s, outs in enumerate(projected):
        for i in range(batch):
            j = s * batch + i
            out_come = lax.ppermute(outs[i], "yl", SWAP)
            out_come = after(out_come, *((a, b) if j else projected[1][2:]))
            a, b = pl.pallas_call(
                combine_kernel,
                name="combine",
                out_shape=[jax.ShapeDtypeStruct((rows, cols // 2), BF16)] * 2,
                in_specs=[VMEM] * 2,
                out_specs=[VMEM] * 2,
                compiler_params=PARAMS,
                cost_estimate=cost(1 << 16, 1 << 16),
            )(outs[batch + i], out_come)
            a = lax.ppermute(a, ("yh", "yl", "core"), across)
            b = lax.ppermute(b, ("yh", "yl", "core"), beside)
            before = [] if result is None else [result]
            part = pl.BlockSpec((rows, cols // 2), lambda i: (0, 0))
            block = pl.BlockSpec((1, rows, cols), lambda i, j=j: (j, 0, 0))
            result = pl.pallas_call(
                functools.partial(finish_kernel, j),
                name="finish",
                grid=(1,),
                out_shape=jax.ShapeDtypeStruct(hidden.shape, BF16),
                in_specs=[block, pl.BlockSpec(out_gate.shape, lambda i: (0, 0)), part, part]
                + [pl.BlockSpec(memory_space=pl.ANY)] * len(before),
                out_specs=block,
                input_output_aliases={4: 0} if before else {},
                compiler_params=PARAMS,
                cost_estimate=cost(1 << 16, 1 << 16),
            )(hidden, out_gate, a, b, *before)
    return result


def solution(mesh):
    split = Mesh(
        mesh.devices.reshape(mesh.shape["segment"], 8, 2, 2, 2), ("x", "z", "yh", "yl", "core")
    )
    return jax.shard_map(
        shards,
        mesh=split,
        in_specs=(
            P(SEQ, None, "x"),
            P(),
            P(),
            P("x"),
            P("x", MP),
            P("x", MP),
            P("x", SEQ, MP),
            P("x", SEQ, MP),
            P("x", MP),
            P(MP, SEQ),
        ),
        out_specs=P("x", SEQ, MP),
        check_vma=False,
    )
```

```python
import functools
import math

import jax
import jax.numpy as jnp
from jax import lax
from jax.experimental import pallas as pl
from jax.experimental.pallas import tpu as pltpu
from jax.sharding import Mesh
from jax.sharding import PartitionSpec as P

HEAD = 128
SEQ = ("z", "yh")
MP = ("yl", "core")
SWAP = [(0, 1), (1, 0)]
VMEM = pl.BlockSpec(memory_space=pltpu.VMEM)
SMEM = pl.BlockSpec(memory_space=pltpu.SMEM)
PARAMS = pltpu.CompilerParams(vmem_limit_bytes=26 * 1024 * 1024)
F32 = jnp.float32
BF16 = jnp.bfloat16


def rotation(count, by):
    return [(k, (k + by) % count) for k in range(count)]


def after(value, *tokens):
    return lax.optimization_barrier((value, *tokens))[0]


def cost(flops, moved):
    return pl.CostEstimate(flops=flops, bytes_accessed=moved, transcendentals=0)


def ring_of(value, count, *beside):
    half = count // 2
    ring = [value] + [None] * (count - 1)
    for k in range(1, half + 1):
        if k == half:
            ring[k - 1] = after(ring[k - 1], *beside)
        ring[k] = lax.ppermute(ring[k - 1], "z", rotation(count, 1))
        if k < half:
            ring[count - k] = lax.ppermute(ring[(count - k + 1) % count], "z", rotation(count, -1))
    return ring


def project_kernel(nx, owner_ref, pieces_ref, gain_ref, wk_ref, wv_ref, *rest):
    outs, (scaled, scratch) = rest[:nx], rest[nx:]
    captions, slots, share = pieces_ref.shape
    step, steps = pl.program_id(0), pl.num_programs(0)
    block = wk_ref.shape[1]
    cols = (scratch.shape[1] - HEAD) // 2

    @pl.when(step == 0)
    def _():
        rows = pieces_ref[...].reshape(captions * slots, share).astype(F32)
        squares = jnp.sum(rows * rows, axis=1, keepdims=True)
        high = squares.astype(BF16).astype(F32)
        low = squares - high
        lane = lax.broadcasted_iota(jnp.int32, (captions * slots, HEAD), 1)
        tail = jnp.where(lane == 0, high, jnp.where(lane == 1, low, 0.0))
        scratch[:, 2 * cols :] = tail.astype(BF16)
        scaled[...] = (rows * gain_ref[...]).astype(BF16)

    for ref, offset in ((wk_ref, 0), (wv_ref, cols)):
        at = pl.ds(pl.multiple_of(offset + step * block, block), block)
        scratch[:, at] = jnp.dot(scaled[...], ref[...], preferred_element_type=F32).astype(BF16)

    @pl.when(step == steps - 1)
    def _():
        x = lax.axis_index("x")
        images = outs[0].shape[0]
        for r in range(nx):
            there = lax.rem(x + r, nx)
            for j in range(images):
                caption = owner_ref[there * images + j]
                start = pl.multiple_of(caption * slots, slots)
                outs[r][j] = scratch[pl.ds(start, slots), :]


def add_kernel(width, *refs):
    parts, out_ref = refs[:-1], refs[-1]
    wide = parts[0].shape[2]
    cols = (wide - HEAD) // 2
    total = parts[0][...].astype(F32)
    for p in parts[1:]:
        total = total + p[...].astype(F32)
    squares = total[:, :, 2 * cols : 2 * cols + 1] + total[:, :, 2 * cols + 1 : 2 * cols + 2]
    scale = lax.rsqrt(squares / width + 1e-06)
    keys = total[:, :, :cols] * (scale * (HEAD**-0.5 * math.log2(math.e)))
    out_ref[:, :, :cols] = keys.astype(BF16)
    out_ref[:, :, cols:] = (total[:, :, cols : 2 * cols] * scale).astype(BF16)


def attend_kernel(first, total, nz, owner_ref, length_ref, mine_ref, theirs_ref, *rest):
    pieces, (keep_ref, send_ref) = rest[:nz], rest[nz:]
    core, z = lax.axis_index("core"), lax.axis_index("z")
    rows, cols = mine_ref.shape[1:]
    slots = pieces[0].shape[1]
    image = lax.axis_index("x") * total + first + pl.program_id(0)
    live = length_ref[owner_ref[image]]
    lane = lax.broadcasted_iota(jnp.int32, (2 * rows, HEAD), 1)
    slot = lax.rem(z + nz - lane // slots, nz) * slots + lax.rem(lane, slots)
    dead = slot >= live

    for h in range(cols // HEAD):
        at = slice(h * HEAD, (h + 1) * HEAD)
        there = slice(cols + h * HEAD, cols + (h + 1) * HEAD)
        mine, theirs = mine_ref[0, :, at], theirs_ref[0, :, at]
        q = jnp.concatenate(
            [jnp.where(core == 0, mine, theirs), jnp.where(core == 0, theirs, mine)], axis=0
        )
        keys = jnp.concatenate([p[0, :, at] for p in pieces], axis=0)
        values = jnp.concatenate([p[0, :, there] for p in pieces], axis=0)
        scores = lax.dot_general(q, keys, (((1,), (1,)), ((), ())), preferred_element_type=F32)
        scores = jnp.where(dead, -1e30, scores)
        top = jnp.max(scores, axis=1, keepdims=True)
        raised = jnp.exp2(scores - top)
        weights = (raised / jnp.sum(raised, axis=1, keepdims=True)).astype(BF16)
        out = jnp.dot(weights, values, preferred_element_type=F32).astype(BF16)
        keep_ref[:, at] = out[:rows]
        send_ref[:, at] = out[rows:]


def output_kernel(nx, nz, order_ref, keep_ref, come_ref, *rest):
    sides, outs, (held, sems) = (rest[:5], rest[5:10]), rest[10:-2], rest[-2:]
    sends, stays = outs[: len(outs) // 2], outs[len(outs) // 2 :]
    x = lax.axis_index("x")
    core, yl = lax.axis_index("core"), lax.axis_index("yl")
    deep, wide = rest[0].shape[1:]
    sent_block = jnp.where(core == 0, 1 - yl, yl)
    half = nz // 2

    copies = []
    for first in range(2):
        span = pl.ds(first * half, half)
        group = []
        for side in range(2):
            for part in range(nx):
                ref = sides[side][part].at[span] if part < nx - 1 else sides[side][part + first]
                row = pl.ds((side * nx + part) * deep, deep)
                group.append(
                    pltpu.make_async_copy(ref, held.at[span, row], sems.at[first, side, part])
                )
        copies.append(group)
    for group in copies:
        for copy in group:
            copy.start()

    slabs = []
    for ref in (keep_ref, come_ref):
        for r in (0, 1, nx - 1, 2):
            start = pl.multiple_of(lax.rem(x + nx - r, nx) * deep, deep)
            slabs.append(ref[:, pl.ds(start, deep)])
    left = jnp.concatenate(slabs, axis=1)

    def column(k):
        out = jnp.dot(left, held[k], preferred_element_type=F32).astype(BF16)
        there = k
        start = pl.multiple_of(lax.rem(there, half) * wide, wide)

        rows = sends[0].shape[0]

        @pl.when(there // half == sent_block)
        def _():
            for i, ref in enumerate(sends):
                ref[:, pl.ds(start, wide)] = out[i * rows : (i + 1) * rows]

        @pl.when(there // half != sent_block)
        def _():
            for i, ref in enumerate(stays):
                ref[:, pl.ds(start, wide)] = out[i * rows : (i + 1) * rows]

    for first in range(2):
        for copy in copies[first]:
            copy.wait()

        @pl.loop(0, half)
        def _(k):
            column(first * half + k)


def combine_kernel(stay_ref, come_ref, a_ref, b_ref):
    core = lax.axis_index("core")
    half = a_ref.shape[1]
    for ref, which in ((a_ref, 1 - core), (b_ref, core)):
        at = pl.ds(pl.multiple_of(which * half, half), half)
        ref[...] = (stay_ref[:, at].astype(F32) + come_ref[:, at].astype(F32)).astype(BF16)


def finish_kernel(image, hidden_ref, gate_ref, a_ref, b_ref, *rest):
    out_ref = rest[-1]
    core, yh = lax.axis_index("core"), lax.axis_index("yh")
    second = lax.rem(yh + core, 2)
    wide = a_ref.shape[1] // 2
    for ref, parity in ((a_ref, 1 - second), (b_ref, second)):
        for k in range(2):
            at = pl.ds(pl.multiple_of((2 * k + parity) * wide, wide), wide)
            part = ref[:, k * wide : (k + 1) * wide].astype(F32)
            out = hidden_ref[0, :, at].astype(F32) + gate_ref[image : image + 1, at] * part
            out_ref[0, :, at] = out.astype(BF16)


def shards(
    captions,
    caption_lengths,
    image_caption,
    t5_gain,
    w_key,
    w_value,
    queries,
    hidden,
    out_gate,
    w_out,
):
    nx, nz, nh = lax.axis_size("x"), lax.axis_size("z"), lax.axis_size("yh")
    _, slots, share = captions.shape
    images, rows, cols = queries.shape
    deep, wide = w_out.shape
    slot_share = slots // nz
    caption_count = nz * nh

    cut = captions.reshape(nz, 1, slot_share, share)
    cut = jnp.broadcast_to(cut, (nz, nh, slot_share, share))
    cut = cut.reshape(caption_count, slot_share, share)
    pieces = lax.all_to_all(cut, SEQ, 0, 0, tiled=True)

    theirs = lax.ppermute(after(queries, cut), "yh", SWAP)
    quarter = deep // nx
    mine = lax.dynamic_slice_in_dim(
        after(w_out, cut), lax.axis_index("x") * quarter, quarter, 0
    )
    w_z = lax.all_to_all(
        jnp.broadcast_to(mine[None], (nz, *mine.shape)), "z", 0, 0, tiled=True
    )

    partial = pl.pallas_call(
        functools.partial(project_kernel, nx),
        name="project",
        grid=(4,),
        out_shape=[jax.ShapeDtypeStruct((images, slot_share, 2 * cols + HEAD), BF16)] * nx,
        in_specs=[
            SMEM,
            pl.BlockSpec(pieces.shape, lambda i: (0, 0, 0)),
            pl.BlockSpec((1, share), lambda i: (0, 0)),
            pl.BlockSpec((share, cols // 4), lambda i: (0, i)),
            pl.BlockSpec((share, cols // 4), lambda i: (0, i)),
        ],
        out_specs=[
            pl.BlockSpec((images, slot_share, 2 * cols + HEAD), lambda i: (0, 0, 0))
        ]
        * nx,
        scratch_shapes=[
            pltpu.VMEM((caption_count * slot_share, share), BF16),
            pltpu.VMEM((caption_count * slot_share, 2 * cols + HEAD), BF16),
        ],
        compiler_params=pltpu.CompilerParams(vmem_limit_bytes=58 * 1024 * 1024),
        cost_estimate=cost(4 * caption_count * slot_share * share * cols, 6 << 20),
    )(image_caption, pieces, t5_gain.reshape(1, share), w_key, w_value)
    arrived = [partial[0]] + [
        lax.ppermute(partial[r], "x", rotation(nx, r)) for r in range(1, nx)
    ]
    stream = pl.pallas_call(
        functools.partial(add_kernel, float(share * nx)),
        name="add",
        out_shape=jax.ShapeDtypeStruct((images, slot_share, 2 * cols), BF16),
        in_specs=[VMEM] * nx,
        out_specs=VMEM,
        compiler_params=PARAMS,
        cost_estimate=cost(1 << 16, 1 << 16),
    )(*arrived)
    w_x = after(w_z, stream)
    ahead = lax.ppermute(w_x, "x", rotation(nx, 1))
    back = lax.ppermute(w_x, "x", rotation(nx, -1))
    ring = ring_of(stream, nz)
    ahead, back = after(ahead, ring[5]), after(back, ring[5])
    far = [
        lax.ppermute(ahead[: nz // 2], "x", rotation(nx, 1)),
        lax.ppermute(back[nz // 2 :], "x", rotation(nx, -1)),
    ]
    w_mine = [w_x, ahead, back, *far]

    across = [(h * 4 + l * 2, h * 4 + l * 2 + 1) for h in range(2) for l in range(2)]
    across += [(h * 4 + l * 2 + 1, (1 - h) * 4 + (1 - l) * 2) for h in range(2) for l in range(2)]
    beside = [(h * 4 + l * 2, h * 4 + l * 2) for h in range(2) for l in range(2)]
    beside += [
        (h * 4 + l * 2 + 1, (1 - h) * 4 + (1 - l) * 2 + 1) for h in range(2) for l in range(2)
    ]

    result, projected = None, []
    batch = images // 2
    for s in range(2):
        block = pl.BlockSpec((1, rows, cols), lambda i, s=s: (s * batch + i, 0, 0))
        piece = pl.BlockSpec((1, slot_share, 2 * cols), lambda i, s=s: (s * batch + i, 0, 0))
        flat = pl.BlockSpec((rows, cols), lambda i: (i, 0))
        keep, send = pl.pallas_call(
            functools.partial(attend_kernel, s * batch, images, nz),
            name="attend",
            grid=(batch,),
            out_shape=[jax.ShapeDtypeStruct((batch * rows, cols), BF16)] * 2,
            in_specs=[SMEM, SMEM, block, block] + [piece] * nz,
            out_specs=[flat, flat],
            compiler_params=PARAMS,
            cost_estimate=cost(1 << 16, 1 << 16),
        )(
            after(image_caption, *(far if s else (ahead, back))),
            caption_lengths,
            queries,
            theirs,
            *ring,
        )
        come = lax.ppermute(send, "core", SWAP)
        if not s:
            w_theirs = [lax.ppermute(after(w, keep), "core", SWAP) for w in w_mine]
        outs = pl.pallas_call(
            functools.partial(output_kernel, nx, nz),
            name="output",
            out_shape=[jax.ShapeDtypeStruct((rows, nz // 2 * wide), BF16)] * (2 * batch),
            in_specs=[SMEM, VMEM, VMEM] + [pl.BlockSpec(memory_space=pl.ANY)] * 10,
            out_specs=[VMEM] * (2 * batch),
            scratch_shapes=[
                pltpu.VMEM((nz, 2 * deep, wide), BF16),
                pltpu.SemaphoreType.DMA((2, 2, nx)),
            ],
            compiler_params=PARAMS,
            cost_estimate=cost(1 << 16, 1 << 16),
        )(image_caption, keep, come, *w_mine, *w_theirs)
        projected.append(outs)
    for s, outs in enumerate(projected):
        for i in range(batch):
            j = s * batch + i
            out_come = lax.ppermute(outs[i], "yl", SWAP)
            out_come = after(out_come, *((a, b) if j else projected[1][2:]))
            a, b = pl.pallas_call(
                combine_kernel,
                name="combine",
                out_shape=[jax.ShapeDtypeStruct((rows, cols // 2), BF16)] * 2,
                in_specs=[VMEM] * 2,
                out_specs=[VMEM] * 2,
                compiler_params=PARAMS,
                cost_estimate=cost(1 << 16, 1 << 16),
            )(outs[batch + i], out_come)
            a = lax.ppermute(a, ("yh", "yl", "core"), across)
            b = lax.ppermute(b, ("yh", "yl", "core"), beside)
            before = [] if result is None else [result]
            part = pl.BlockSpec((rows, cols // 2), lambda i: (0, 0))
            block = pl.BlockSpec((1, rows, cols), lambda i, j=j: (j, 0, 0))
            result = pl.pallas_call(
                functools.partial(finish_kernel, j),
                name="finish",
                grid=(1,),
                out_shape=jax.ShapeDtypeStruct(hidden.shape, BF16),
                in_specs=[block, pl.BlockSpec(out_gate.shape, lambda i: (0, 0)), part, part]
                + [pl.BlockSpec(memory_space=pl.ANY)] * len(before),
                out_specs=block,
                input_output_aliases={4: 0} if before else {},
                compiler_params=PARAMS,
                cost_estimate=cost(1 << 16, 1 << 16),
            )(hidden, out_gate, a, b, *before)
    return result


def solution(mesh):
    split = Mesh(
        mesh.devices.reshape(mesh.shape["segment"], 8, 2, 2, 2), ("x", "z", "yh", "yl", "core")
    )
    return jax.shard_map(
        shards,
        mesh=split,
        in_specs=(
            P(SEQ, None, "x"),
            P(),
            P(),
            P("x"),
            P("x", MP),
            P("x", MP),
            P("x", SEQ, MP),
            P("x", SEQ, MP),
            P("x", MP),
            P(MP, SEQ),
        ),
        out_specs=P("x", SEQ, MP),
        check_vma=False,
    )
```
